32 devices in a mesh: tm: 16 (over z, y, x), head: 2 (over core).
Axes of the slice: x: 2, y: 2, z: 4, core: 2. Of those that a mesh axis runs over, the one named last changes fastest.
Arguments:
- patches: bfloat16 [192, 256, 1152], P('tm', None, 'head'), may hold values from -6 to 6
- grid_rows: int32 [192], P('tm'), may hold values from 8 to 16
- frame_ids: int32 [192], P('tm'), may hold values from 0 to 191, as said below
- ln_gain: float32 [1152], replicated, may hold values from 0.1 to 1.9
- w_qkv: bfloat16 [3, 1152, 1152], P(None, None, 'head'), may hold values from -5.9514821 to 5.9514821
- w_out: bfloat16 [1152, 1152], P('head'), may hold values from -0.1875 to 0.1875
- w_conn: bfloat16 [1152, 4096], P(None, 'head'), may hold values from -0.1875 to 0.1875
- norm_gain: float32 [4096], replicated, may hold values from 0.1 to 1.9
- w_x: bfloat16 [4096, 4096], P(None, 'head'), may hold values from -0.09375 to 0.09375
- w_b: bfloat16 [4096, 1024], P(None, 'head'), may hold values from -0.09375 to 0.09375
- w_c: bfloat16 [4096, 1024], P(None, 'head'), may hold values from -0.09375 to 0.09375
- w_dt: bfloat16 [4096, 64], P(None, 'head'), may hold values from -0.09375 to 0.09375
- dt_bias: float32 [64], P('head'), may hold values from -1 to 1
- a_log: float32 [64], P('head'), may hold values from -14 to -3.2
- d_skip: float32 [64], P('head'), may hold values from 0.5 to 1.5
- out_gain: float32 [4096], P('head'), may hold values from 0.1 to 1.9
Outputs:
- stream: bfloat16 [12288, 4096], P('tm', 'head')
- ssd_out: bfloat16 [12288, 4096], P('tm', 'head')
The draws below stay inside these ranges and needn't reach their ends.
Inputs may be any that keep to these rules, and one draw needn't show every extreme that they name: frame_ids is a permutation of the frames; the 12 slots of one tm index hold frames of 12 different time shards, time shard of a frame being frame // 12.
All inputs are finite; a program needn't handle non-finite values.
Results may differ from the reference program's by a relative error of at most 0.013.
Values may be sent and summed in bfloat16 or wider, within the bound.
A program may use at most 128 MiB of HBM per device.

```python
import math
import jax
import jax.numpy as jnp
from jax import lax

GRID = 16
POOL = 4
P_SIZE = 256
PT = 64
VHEADS = 16
VHD = 72
DV = 1152
D = 4096
HEADS = 64
HDIM = 64
STATE = 128
GROUPS = 8
FR_DEV = 12
FRAMES = 192
TOKENS = 12288
STRETCH = 256
N_TM = 16


def draw_frame_ids(key, part):
    offset_key, owner_key, order_key, slot_key = jax.random.split(key, 4)
    offsets = jax.random.permutation(offset_key, N_TM)[:FR_DEV]
    owners = jax.random.permutation(owner_key, N_TM)
    within = jax.vmap(lambda subkey: jax.random.permutation(subkey, FR_DEV))(jax.random.split(order_key, N_TM))
    slot_order = jax.vmap(lambda subkey: jax.random.permutation(subkey, FR_DEV))(jax.random.split(slot_key, N_TM))
    sender = jnp.arange(N_TM)[:, None]
    column = jnp.broadcast_to(jnp.arange(FR_DEV)[None, :], (N_TM, FR_DEV))
    target = (sender + offsets[None, :]) % N_TM
    frames = target * FR_DEV + within[target, column]
    placed = jnp.zeros((N_TM, FR_DEV), jnp.int32).at[jnp.broadcast_to(owners[:, None], (N_TM, FR_DEV)), slot_order].set(frames.astype(jnp.int32))
    return placed.reshape(N_TM * FR_DEV)


def draw_w_qkv(key, part):
    base = jnp.clip(jax.random.normal(key, (3, DV, DV), jnp.float32), -5.0, 5.0) * DV ** (-0.5)
    return base.astype(jnp.bfloat16)


def draw_a_log(key, part):
    pick_key, fast_key, slow_key = jax.random.split(key, 3)
    fast_share = 5
    fast = jax.random.randint(pick_key, (HEADS,), 0, 10) < fast_share
    quick = jax.random.uniform(fast_key, (HEADS,), jnp.float32, math.log(1.0 / 50.0), math.log(1.0 / 25.0))
    gentle = jax.random.uniform(slow_key, (HEADS,), jnp.float32, math.log(0.2), math.log(2.0)) - math.log(TOKENS)
    return jnp.where(fast, quick, gentle)


def place_ends(array, rng, least, high):
    longest = array.shape.index(max(array.shape))
    spots = []
    for shift in (0, 1):
        where = [jax.random.randint(jax.random.fold_in(rng, axis), (), 0, length) for axis, length in enumerate(array.shape)]
        where[longest] = (where[longest] + shift) % array.shape[longest]
        spots.append(tuple(where))
    return array.at[spots[0]].set(least).at[spots[1]].set(high)


def levels(stream_key, dims, cuts, smallest, largest):
    loudness, own = 1.0, jax.random.fold_in(stream_key, 6)
    for position, parts in cuts:
        heights = jnp.exp(jax.random.uniform(jax.random.fold_in(own, position), (parts,), jnp.float32, smallest / len(cuts), largest / len(cuts)))
        loudness = loudness * jnp.repeat(heights, dims[position] // parts).reshape([-1 if axis == position else 1 for axis in range(len(dims))])
    return loudness


def gaussian(own_key, dims, deviation, limit, cuts=(), kind=jnp.bfloat16):
    level = levels(own_key, dims, cuts, -0.22, 0.18) if cuts else 1.0
    result = jax.random.normal(own_key, dims, jnp.float32) * deviation * level
    return jnp.minimum(jnp.maximum(result, -limit), limit).astype(kind)


def setup_inputs(seed: int = 0) -> dict:
    seeds = jax.random.split(jax.random.key(seed), 17)
    patches = gaussian(seeds[0], (FRAMES, P_SIZE, DV), 1.0, 6.0, ((0, 16), (2, 2)))
    grid_rows = place_ends(jax.random.randint(seeds[1], (FRAMES,), GRID // 2, GRID + 1), jax.random.fold_in(seeds[1], 1), GRID // 2, GRID).astype(jnp.int32)
    frame_ids = draw_frame_ids(jax.random.fold_in(seeds[16], 71), 0)
    ln_gain = jnp.clip(1.0 + 0.18 * jax.random.normal(seeds[3], (DV,), jnp.float32), 0.1, 1.9)
    w_qkv = draw_w_qkv(jax.random.fold_in(seeds[16], 71), 0)
    w_out = gaussian(seeds[5], (DV, DV), DV ** -0.5, 0.1875, ((0, 2),))
    w_conn = gaussian(seeds[6], (DV, D), DV ** -0.5, 0.1875, ((1, 2),))
    norm_gain = jnp.clip(1.0 + 0.18 * jax.random.normal(seeds[7], (D,), jnp.float32), 0.1, 1.9)
    w_x = gaussian(seeds[8], (D, HEADS * HDIM), D ** -0.5, 0.09375, ((1, 2),))
    w_b = gaussian(seeds[9], (D, GROUPS * STATE), D ** -0.5, 0.09375, ((1, 2),))
    w_c = gaussian(seeds[10], (D, GROUPS * STATE), D ** -0.5, 0.09375, ((1, 2),))
    w_dt = gaussian(seeds[11], (D, HEADS), D ** -0.5, 0.09375, ((1, 2),))
    dt_bias = jnp.clip(jax.random.uniform(seeds[12], (HEADS,), jnp.float32, -1.0, 1.0) * levels(seeds[12], (HEADS,), ((0, 2),), -0.4, 0.0), -1.0, 1.0)
    a_log = draw_a_log(jax.random.fold_in(seeds[16], 71), 0)
    d_skip = jnp.clip(0.5 + 1.0 * jax.random.uniform(seeds[14], (HEADS,), jnp.float32) ** levels(seeds[14], (HEADS,), ((0, 2),), -0.2, 0.2), 0.5, 1.5)
    out_gain = jnp.clip(1.0 + 0.18 * jax.random.normal(seeds[15], (HEADS * HDIM,), jnp.float32), 0.1, 1.9)
    return dict(patches=patches, grid_rows=grid_rows, frame_ids=frame_ids, ln_gain=ln_gain, w_qkv=w_qkv, w_out=w_out, w_conn=w_conn, norm_gain=norm_gain, w_x=w_x, w_b=w_b, w_c=w_c, w_dt=w_dt, dt_bias=dt_bias, a_log=a_log, d_skip=d_skip, out_gain=out_gain)


highest = lax.Precision.HIGHEST

def layer_norm(rows, gain):
    values = rows.astype(jnp.float32)
    centre = lax.optimization_barrier(jnp.mean(values, axis=-1, keepdims=True))
    spread = lax.optimization_barrier(jnp.mean(jnp.square(values - centre), axis=-1, keepdims=True))
    return ((values - centre) * lax.rsqrt(spread + 1e-06) * gain).astype(jnp.bfloat16)

def vision_frames(frames, grid_rows, ln_gain, w_qkv, w_out):
    frame_count = frames.shape[0]
    normed = layer_norm(frames, ln_gain).reshape(frame_count * P_SIZE, DV)
    queries, keys_all, values_all = [jnp.dot(normed, w_qkv[member], preferred_element_type=jnp.float32).astype(jnp.bfloat16).reshape(frame_count, P_SIZE, VHEADS, VHD) for member in range(3)]
    scores = jnp.einsum('fqhd,fkhd->fhqk', queries.astype(jnp.float32), keys_all.astype(jnp.float32)) * VHD ** (-0.5)
    valid_count = grid_rows * GRID
    usable = jnp.arange(P_SIZE)[None, :] < valid_count[:, None]
    scores = jnp.where(usable[:, None, None, :], scores, -1e+30)
    row_max = lax.optimization_barrier(jnp.max(scores, axis=-1, keepdims=True))
    powered = jnp.exp(scores - row_max)
    weights_soft = (powered / lax.optimization_barrier(jnp.sum(powered, axis=-1, keepdims=True))).astype(jnp.bfloat16)
    context = jnp.einsum('fhqk,fkhd->fqhd', weights_soft.astype(jnp.float32), values_all.astype(jnp.float32)).astype(jnp.bfloat16)
    attended = jnp.dot(context.reshape(frame_count * P_SIZE, DV), w_out, preferred_element_type=jnp.float32)
    summed = frames.astype(jnp.float32).reshape(frame_count * P_SIZE, DV) + attended
    pooled = lax.optimization_barrier(jnp.mean(summed.reshape(frame_count, PT, POOL, DV), axis=2))
    kept_tokens = jnp.arange(PT)[None, :] * POOL < valid_count[:, None]
    return jnp.where(kept_tokens[:, :, None], pooled, 0.0).astype(jnp.bfloat16)

def project(stream_rows, norm_gain, w_x, w_b, w_c, w_dt, dt_bias, a_log):
    values = stream_rows.astype(jnp.float32)
    normed = (values * lax.rsqrt(lax.optimization_barrier(jnp.mean(values * values, axis=-1, keepdims=True)) + 1e-05) * norm_gain).astype(jnp.bfloat16)
    inner_rows = jnp.dot(normed, w_x, preferred_element_type=jnp.float32).astype(jnp.bfloat16)
    write_keys = jnp.dot(normed, w_b, preferred_element_type=jnp.float32).astype(jnp.bfloat16)
    read_keys = jnp.dot(normed, w_c, preferred_element_type=jnp.float32).astype(jnp.bfloat16)
    step_size = jax.nn.softplus(jnp.dot(normed, w_dt, preferred_element_type=jnp.float32) + dt_bias)
    log_decay = -jnp.exp(a_log) * step_size
    return (inner_rows, write_keys, read_keys, step_size, log_decay)

def ssd_stretch(inner_rows, write_keys, read_keys, step_size, log_decay, d_skip, state):
    length = inner_rows.shape[0]
    head_count = step_size.shape[1]
    groups = write_keys.shape[1] // STATE
    per_group = head_count // groups
    cumul = jnp.cumsum(log_decay, axis=0)
    scaled = inner_rows.astype(jnp.float32).reshape(length, head_count, HDIM) * step_size[:, :, None]
    writers = write_keys.astype(jnp.float32).reshape(length, groups, STATE)
    readers = read_keys.astype(jnp.float32).reshape(length, groups, STATE)
    intersection = jnp.einsum('tgn,sgn->gts', readers, writers, precision=highest)
    causal = (jnp.arange(length)[:, None] >= jnp.arange(length)[None, :])[:, :, None]
    spans = cumul[:, None, :] - cumul[None, :, :]
    decays = jnp.where(causal, jnp.exp(jnp.where(causal, spans, 0.0)), 0.0)
    mixing = jnp.repeat(intersection, per_group, axis=0) * jnp.transpose(decays, (2, 0, 1))
    within = jnp.einsum('hts,shp->thp', mixing, scaled, precision=highest)
    carried = jnp.einsum('tgn,gkpn->tgkp', readers, state.reshape(groups, per_group, HDIM, STATE), precision=highest).reshape(length, head_count, HDIM) * jnp.exp(cumul)[:, :, None]
    remaining = jnp.exp(cumul[-1][None, :] - cumul)
    fresh_state = jnp.einsum('sgkp,sgn->gkpn', (scaled * remaining[:, :, None]).reshape(length, groups, per_group, HDIM), writers, precision=highest).reshape(head_count, HDIM, STATE)
    new_state = jnp.exp(cumul[-1])[:, None, None] * state + fresh_state
    outputs = within + carried + d_skip[None, :, None] * inner_rows.astype(jnp.float32).reshape(length, head_count, HDIM)
    return (outputs, new_state, cumul)

def group_norm(outputs, out_gain, groups):
    length = outputs.shape[0]
    grouped = outputs.reshape(length, groups, -1)
    normed = grouped * lax.rsqrt(lax.optimization_barrier(jnp.mean(grouped * grouped, axis=-1, keepdims=True)) + 1e-05)
    return (normed.reshape(length, -1) * out_gain).astype(jnp.bfloat16)

def reference(patches, grid_rows, frame_ids, ln_gain, w_qkv, w_out, w_conn, norm_gain, w_x, w_b, w_c, w_dt, dt_bias, a_log, d_skip, out_gain):

    def vision_block(block_id):
        first = (block_id * FR_DEV).astype(jnp.int32)
        frames = lax.dynamic_slice_in_dim(patches, first, FR_DEV, 0)
        rows_valid = lax.dynamic_slice_in_dim(grid_rows, first, FR_DEV, 0)
        return vision_frames(frames, rows_valid, ln_gain, w_qkv, w_out)
    owned = lax.map(vision_block, jnp.arange(FRAMES // FR_DEV, dtype=jnp.int32)).reshape(FRAMES, PT, DV)
    placement = jnp.zeros((FRAMES,), jnp.int32).at[frame_ids].set(jnp.arange(FRAMES, dtype=jnp.int32))
    in_time = owned[placement].reshape(TOKENS, DV)
    stream = jnp.dot(in_time, w_conn, preferred_element_type=jnp.float32).astype(jnp.bfloat16)

    def stretch_step(state, rows):
        inner_rows, write_keys, read_keys, step_size, log_decay = project(rows, norm_gain, w_x, w_b, w_c, w_dt, dt_bias, a_log)
        outputs, new_state, cumul = ssd_stretch(inner_rows, write_keys, read_keys, step_size, log_decay, d_skip, state)
        return (new_state, group_norm(outputs, out_gain, GROUPS))
    zero_state = jnp.zeros((HEADS, HDIM, STATE), jnp.float32)
    final_state, mixed = lax.scan(stretch_step, zero_state, stream.reshape(TOKENS // STRETCH, STRETCH, D))
    return (stream, mixed.reshape(TOKENS, HEADS * HDIM))
```

```python
import functools
import math

import jax
import jax.numpy as jnp
from jax import lax
from jax.experimental import pallas as pl
from jax.experimental.pallas import tpu as pltpu
from jax.sharding import PartitionSpec as P

GRID = 16
POOL = 4
VHD = 72
HDIM = 64
STATE = 128
CHUNK = 128
LANES = 128

f32 = jnp.float32
bf16 = jnp.bfloat16
VMEM = pltpu.VMEM
CONTRACT_LAST = (((1,), (1,)), ((), ()))
CONTRACT_FIRST = (((0,), (0,)), ((), ()))


def attend_kernel(
    valid_ref, my_ref, full_ref, own_ref, gain_ref, wqkv_ref, wout_ref, out_ref, normed, context
):
    parts, _, patch_count, part_width = full_ref.shape
    full_width = parts * part_width
    local_width = wqkv_ref.shape[2]
    tokens = patch_count // POOL
    frame = pl.program_id(0)
    pieces = [full_ref[part, 0].astype(f32) for part in range(parts)]
    centre = sum(jnp.sum(piece, axis=-1, keepdims=True) for piece in pieces) / full_width
    pieces = [piece - centre for piece in pieces]
    spread = sum(jnp.sum(piece * piece, axis=-1, keepdims=True) for piece in pieces) / full_width
    scale = lax.rsqrt(spread + 1e-06)
    for part in range(parts):
        normed[:, part * part_width : (part + 1) * part_width] = (
            pieces[part] * scale * gain_ref[part]
        ).astype(bf16)
    rows = normed[...]
    queries, keys, values = [
        jnp.dot(rows, wqkv_ref[member], preferred_element_type=f32).astype(bf16)
        for member in range(3)
    ]
    key_spot = lax.broadcasted_iota(jnp.int32, (1, patch_count), 1)
    bias = jnp.where(key_spot < valid_ref[frame], 0.0, -1e30).astype(f32)
    factor = VHD ** (-0.5) * math.log2(math.e)
    for head in range(local_width // VHD):
        at = slice(head * VHD, (head + 1) * VHD)
        scores = (
            lax.dot_general(
                queries[:, at], keys[:, at], CONTRACT_LAST, preferred_element_type=f32
            )
            + bias
        )
        powered = jnp.exp2((scores - jnp.max(scores, axis=-1, keepdims=True)) * factor)
        total = jnp.sum(powered, axis=-1, keepdims=True)
        mixed = jnp.dot(powered.astype(bf16), values[:, at], preferred_element_type=f32)
        context[:, at] = (mixed / total).astype(bf16)
    row = lax.broadcasted_iota(jnp.int32, (tokens, patch_count), 0)
    column = lax.broadcasted_iota(jnp.int32, (tokens, patch_count), 1)
    pooling = jnp.where(column // POOL == row, 1.0 / POOL, 0.0).astype(bf16)
    pooled = jnp.dot(pooling, context[...], preferred_element_type=f32).astype(bf16)
    own = jnp.dot(pooling, own_ref[0], preferred_element_type=f32)
    attended = jnp.dot(pooled, wout_ref[...], preferred_element_type=f32)
    for part in range(parts):
        block = attended[:, part * part_width : (part + 1) * part_width]
        out_ref[part, 0] = (block + jnp.where(my_ref[0] == part, own, 0.0)).astype(bf16)


def attend(full, own, valid_count, my, ln_gain, w_qkv, w_out):
    parts, frames, patch_count, part_width = full.shape
    width = parts * part_width
    local_width = w_qkv.shape[2]
    tokens = patch_count // POOL
    return pl.pallas_call(
        attend_kernel,
        out_shape=jax.ShapeDtypeStruct((parts, frames, tokens, part_width), bf16),
        grid_spec=pltpu.PrefetchScalarGridSpec(
            num_scalar_prefetch=2,
            grid=(frames,),
            in_specs=[
                pl.BlockSpec((parts, 1, patch_count, part_width), lambda f, *_: (0, f, 0, 0)),
                pl.BlockSpec((1, patch_count, part_width), lambda f, *_: (f, 0, 0)),
                pl.BlockSpec((parts, 1, part_width), lambda f, *_: (0, 0, 0)),
                pl.BlockSpec((3, width, local_width), lambda f, *_: (0, 0, 0)),
                pl.BlockSpec((local_width, width), lambda f, *_: (0, 0)),
            ],
            out_specs=pl.BlockSpec((parts, 1, tokens, part_width), lambda f, *_: (0, f, 0, 0)),
            scratch_shapes=[
                VMEM((patch_count, width), bf16),
                VMEM((patch_count, local_width), bf16),
            ],
        ),
        name="attend",
    )(valid_count, my, full, own, ln_gain.reshape(parts, 1, part_width), w_qkv, w_out)


def bucket_kernel(slot_ref, label_ref, count_ref, parts_ref, out_ref):
    parts, _, tokens, part_width = parts_ref.shape
    padded = out_ref.shape[2]
    spot = lax.broadcasted_iota(jnp.int32, (tokens, part_width), 0) * POOL

    def step(target, carry):
        slot = slot_ref[target]
        total = sum(parts_ref[part, slot].astype(f32) for part in range(parts))
        kept = jnp.where(spot < count_ref[target], total, 0.0)
        out_ref[target, :, :part_width] = kept.astype(bf16)
        out_ref[target, :, part_width:] = jnp.full(
            (tokens, padded - part_width), label_ref[target].astype(f32)
        ).astype(bf16)
        return carry

    lax.fori_loop(0, out_ref.shape[0], step, 0)


def bucket(parts, frame_ids, valid_count, shards):
    frames, tokens, part_width = parts.shape[1:]
    padded = (part_width // LANES + 1) * LANES
    onehot = (frame_ids // frames)[None, :] == jnp.arange(shards)[:, None]
    pick = lambda row: jnp.sum(jnp.where(onehot, row[None, :], 0), axis=1).astype(jnp.int32)
    return pl.pallas_call(
        bucket_kernel,
        out_shape=jax.ShapeDtypeStruct((shards, tokens, padded), bf16),
        in_specs=[pl.BlockSpec(memory_space=pltpu.SMEM)] * 3 + [pl.BlockSpec(memory_space=VMEM)],
        out_specs=pl.BlockSpec(memory_space=VMEM),
        name="bucket",
    )(
        pick(jnp.arange(frames, dtype=jnp.int32)),
        pick(frame_ids % frames + 1),
        pick(valid_count),
        parts,
    )


def connect_kernel(
    sender_ref, my_ref, arrived_ref, weight_ref, gain_ref, stream_ref, normed_ref, rows, wide
):
    parts, _, tokens, _ = arrived_ref.shape
    width, columns = weight_ref.shape[1:]
    part_width = width // parts
    block_frames = rows.shape[0] // tokens
    for spot in range(block_frames):
        sender = sender_ref[pl.program_id(0) * block_frames + spot]
        for part in range(parts):
            rows[
                spot * tokens : (spot + 1) * tokens, part * part_width : (part + 1) * part_width
            ] = arrived_ref[part, sender, :, :part_width]
    squares = 0.0
    for part in range(parts):
        piece = jnp.dot(rows[...], weight_ref[part], preferred_element_type=f32).astype(bf16)

        @pl.when(my_ref[0] == part)
        def _():
            stream_ref[...] = piece

        piece = piece.astype(f32)
        wide[:, part * columns : (part + 1) * columns] = piece
        squares = squares + jnp.sum(piece * piece, axis=-1, keepdims=True)
    scale = lax.rsqrt(squares / (parts * columns) + 1e-05)
    normed_ref[...] = (wide[...] * scale * gain_ref[...]).astype(bf16)


def connect(arrived, senders, my, weights, norm_gain):
    parts, shards, tokens, padded = arrived.shape
    width, columns = weights.shape[1:]
    frames = senders.shape[0]
    block = math.gcd(frames, 4)
    return pl.pallas_call(
        connect_kernel,
        out_shape=(
            jax.ShapeDtypeStruct((frames * tokens, columns), bf16),
            jax.ShapeDtypeStruct((frames * tokens, parts * columns), bf16),
        ),
        grid_spec=pltpu.PrefetchScalarGridSpec(
            num_scalar_prefetch=2,
            grid=(frames // block,),
            in_specs=[
                pl.BlockSpec((parts, shards, tokens, padded), lambda i, *_: (0, 0, 0, 0)),
                pl.BlockSpec((parts, width, columns), lambda i, *_: (0, 0, 0)),
                pl.BlockSpec((1, parts * columns), lambda i, *_: (0, 0)),
            ],
            out_specs=(
                pl.BlockSpec((block * tokens, columns), lambda i, *_: (i, 0)),
                pl.BlockSpec((block * tokens, parts * columns), lambda i, *_: (i, 0)),
            ),
            scratch_shapes=[
                VMEM((block * tokens, width), bf16),
                VMEM((block * tokens, parts * columns), f32),
            ],
        ),
        name="connect",
    )(senders, my, arrived, weights, norm_gain.reshape(1, -1))


def paired(columns, pair, rows):
    lane = lax.broadcasted_iota(jnp.int32, (rows, LANES), 1)
    return jnp.where(
        lane < HDIM, columns[:, 2 * pair : 2 * pair + 1], columns[:, 2 * pair + 1 : 2 * pair + 2]
    )


def final_state_kernel(inner_ref, write_ref, weight_ref, out_ref):
    length, features = inner_ref.shape
    weights = weight_ref[0]
    for pair in range(features // LANES):
        at = slice(pair * LANES, (pair + 1) * LANES)
        scaled = (inner_ref[:, at].astype(f32) * paired(weights, pair, length)).astype(bf16)
        out_ref[at, :] = lax.dot_general(
            scaled, write_ref[...], CONTRACT_FIRST, preferred_element_type=f32
        ).astype(bf16)


def final_state(inner, write, weights):
    length = inner.shape[0]
    groups = weights.shape[0]
    features = inner.shape[1] // groups
    return pl.pallas_call(
        final_state_kernel,
        out_shape=jax.ShapeDtypeStruct((groups * features, STATE), bf16),
        grid=(groups,),
        in_specs=[
            pl.BlockSpec((length, features), lambda g: (0, g)),
            pl.BlockSpec((length, STATE), lambda g: (0, g)),
            pl.BlockSpec((1, length, weights.shape[2]), lambda g: (g, 0, 0)),
        ],
        out_specs=pl.BlockSpec((features, STATE), lambda g: (g, 0)),
        name="final_state",
    )(inner, write, weights)


def local_kernel(
    inner_ref, write_ref, read_ref, down_ref, across_ref, step_ref, left_ref, skip_ref, out_ref, state
):
    length, features = inner_ref.shape

    @pl.when(pl.program_id(1) == 0)
    def _():
        state[...] = jnp.zeros_like(state)

    readers, writers = read_ref[...], write_ref[...]
    crossing = lax.dot_general(readers, writers, CONTRACT_LAST, preferred_element_type=f32)
    causal = lax.broadcasted_iota(jnp.int32, (length, length), 0) >= lax.broadcasted_iota(
        jnp.int32, (length, length), 1
    )
    crossing = jnp.where(causal, crossing, 0.0)
    down, across, steps, left = down_ref[0], across_ref[0], step_ref[0], left_ref[0]
    grown = jnp.exp(down)
    lane = lax.broadcasted_iota(jnp.int32, (length, LANES), 1)
    row = lax.broadcasted_iota(jnp.int32, (LANES, STATE), 0)
    for pair in range(features // LANES):
        at = slice(pair * LANES, (pair + 1) * LANES)
        inner = inner_ref[:, at]
        halves = []
        for head in (2 * pair, 2 * pair + 1):
            spans = jnp.minimum(down[:, head : head + 1] - across[head : head + 1, :], 0.0)
            mixing = crossing * jnp.exp(spans) * steps[head : head + 1, :]
            halves.append(jnp.dot(mixing.astype(bf16), inner, preferred_element_type=f32))
        held = state[at, :]
        carried = lax.dot_general(
            readers, held.astype(bf16), CONTRACT_LAST, preferred_element_type=f32
        )
        inner = inner.astype(f32)
        out_ref[:, at] = (
            jnp.where(lane < HDIM, halves[0], halves[1])
            + carried * paired(grown, pair, length)
            + skip_ref[:, at] * inner
        )
        scaled = (inner * paired(left, pair, length)).astype(bf16)
        last = grown[length - 1 :, :]
        faded = held * jnp.where(
            row < HDIM, last[:, 2 * pair : 2 * pair + 1], last[:, 2 * pair + 1 : 2 * pair + 2]
        )
        state[at, :] = faded + lax.dot_general(
            scaled, writers, CONTRACT_FIRST, preferred_element_type=f32
        )


def local_outputs(inner, write, read, down, across, steps, left, skip):
    length = inner.shape[0]
    groups, _, per_group = down.shape
    features = inner.shape[1] // groups
    tall = pl.BlockSpec((1, CHUNK, per_group), lambda g, c: (g, c, 0))
    flat = pl.BlockSpec((1, per_group, CHUNK), lambda g, c: (g, 0, c))
    return pl.pallas_call(
        local_kernel,
        out_shape=jax.ShapeDtypeStruct(inner.shape, f32),
        grid=(groups, length // CHUNK),
        in_specs=[
            pl.BlockSpec((CHUNK, features), lambda g, c: (c, g)),
            pl.BlockSpec((CHUNK, STATE), lambda g, c: (c, g)),
            pl.BlockSpec((CHUNK, STATE), lambda g, c: (c, g)),
            tall,
            flat,
            flat,
            tall,
            pl.BlockSpec((1, features), lambda g, c: (0, g)),
        ],
        out_specs=pl.BlockSpec((CHUNK, features), lambda g, c: (c, g)),
        scratch_shapes=[VMEM((features, STATE), f32)],
        cost_estimate=pl.CostEstimate(
            flops=20_000_000_000, bytes_accessed=20_000_000, transcendentals=4_000_000
        ),
        name="local_outputs",
    )(inner, write, read, down, across, steps, left, skip)


def prefix_kernel(arrived_ref, decay_ref, out_ref):
    shards, rows, _ = out_ref.shape
    current = jnp.zeros(out_ref.shape[1:], f32)
    for shard in range(shards):
        out_ref[shard] = current.astype(bf16)
        current = decay_ref[shard] * current + arrived_ref[shard, :rows].astype(f32)


def incoming_state(state, row_log, shards):
    rows = state.shape[0] // shards
    room = 8 * LANES
    logs = row_log.reshape(shards, rows)
    high = logs.astype(bf16)
    low = (logs - high.astype(f32)).astype(bf16)
    widen = lambda part: jnp.pad(part, ((0, 0), (0, room - rows))).reshape(shards, 8, LANES)
    outgoing = jnp.concatenate(
        [state.reshape(shards, rows, STATE), widen(high), widen(low)], axis=1
    )
    arrived = lax.all_to_all(outgoing, "tm", split_axis=0, concat_axis=0, tiled=True)
    tail = arrived[:, rows:].astype(f32).reshape(shards, 2, room)[:, :, :rows]
    decay = jnp.exp(tail[:, 0] + tail[:, 1])[:, :, None]
    before = pl.pallas_call(
        prefix_kernel,
        out_shape=jax.ShapeDtypeStruct((shards, rows, STATE), bf16),
        in_specs=[pl.BlockSpec(memory_space=VMEM)] * 2,
        out_specs=pl.BlockSpec(memory_space=VMEM),
        name="prefix",
    )(arrived, decay)
    return lax.all_to_all(before, "tm", split_axis=0, concat_axis=0, tiled=True).reshape(
        shards * rows, STATE
    )


def finish_kernel(local_ref, read_ref, state_ref, grown_ref, gain_ref, out_ref, total):
    length, features = local_ref.shape
    grown = grown_ref[0]
    squares = 0.0
    for pair in range(features // LANES):
        at = slice(pair * LANES, (pair + 1) * LANES)
        carried = lax.dot_general(
            read_ref[...], state_ref[at, :], CONTRACT_LAST, preferred_element_type=f32
        )
        summed = local_ref[:, at] + carried * paired(grown, pair, length)
        total[:, at] = summed
        squares = squares + jnp.sum(summed * summed, axis=-1, keepdims=True)
    scale = lax.rsqrt(squares / features + 1e-05)
    out_ref[...] = (total[...] * scale * gain_ref[...]).astype(bf16)


def finish(local, read, state, grown, out_gain):
    length = local.shape[0]
    groups, _, per_group = grown.shape
    features = local.shape[1] // groups
    block = 2 * CHUNK
    return pl.pallas_call(
        finish_kernel,
        out_shape=jax.ShapeDtypeStruct(local.shape, bf16),
        grid=(groups, length // block),
        in_specs=[
            pl.BlockSpec((block, features), lambda g, c: (c, g)),
            pl.BlockSpec((block, STATE), lambda g, c: (c, g)),
            pl.BlockSpec((features, STATE), lambda g, c: (g, 0)),
            pl.BlockSpec((1, block, per_group), lambda g, c: (g, c, 0)),
            pl.BlockSpec((1, features), lambda g, c: (0, g)),
        ],
        out_specs=pl.BlockSpec((block, features), lambda g, c: (c, g)),
        scratch_shapes=[VMEM((block, features), f32)],
        name="finish",
    )(local, read, state, grown, out_gain.reshape(1, -1))


def on_device(
    patches,
    grid_rows,
    frame_ids,
    ln_gain,
    w_qkv,
    w_out,
    w_conn,
    norm_gain,
    w_x,
    w_b,
    w_c,
    w_dt,
    dt_bias,
    a_log,
    d_skip,
    out_gain,
):
    frame_count, patch_count, part_width = patches.shape
    shards = lax.axis_size("tm")
    my = lax.axis_index("head").astype(jnp.int32).reshape(1)
    full = lax.all_gather(patches, "head")
    all_conn = lax.all_gather(w_conn, "head")
    valid_count = (grid_rows * GRID).astype(jnp.int32)
    parts = attend(full, patches, valid_count, my, ln_gain, w_qkv, w_out)
    parts = lax.all_to_all(parts, "head", split_axis=0, concat_axis=0, tiled=True)
    outgoing = bucket(parts, frame_ids, valid_count, shards)
    incoming = lax.all_to_all(outgoing, "tm", split_axis=0, concat_axis=0, tiled=True)
    labels = incoming[:, 0, part_width].astype(jnp.int32)
    senders = jnp.sum(
        jnp.where(
            labels[None, :] == jnp.arange(1, frame_count + 1)[:, None],
            jnp.arange(shards, dtype=jnp.int32)[None, :],
            0,
        ),
        axis=1,
    ).astype(jnp.int32)
    arrived = lax.all_gather(incoming, "head")
    stream_rows, normed = connect(arrived, senders, my, all_conn, norm_gain)

    tokens = stream_rows.shape[0]
    heads = w_dt.shape[1]
    groups = w_b.shape[1] // STATE
    per_group = heads // groups
    chunks = tokens // CHUNK
    step_size = jax.nn.softplus(jnp.dot(normed, w_dt, preferred_element_type=f32) + dt_bias)
    log_decay = -jnp.exp(a_log) * step_size
    inner = jnp.dot(normed, w_x, preferred_element_type=f32).astype(bf16)
    write = jnp.dot(normed, w_b, preferred_element_type=f32).astype(bf16)
    read = jnp.dot(normed, w_c, preferred_element_type=f32).astype(bf16)

    cumul = jnp.cumsum(log_decay.reshape(chunks, CHUNK, heads), axis=1)
    ends = cumul[:, -1, :]
    offsets = jnp.cumsum(ends, axis=0) - ends
    total_log = jnp.sum(ends, axis=0)
    from_start = (cumul + offsets[:, None, :]).reshape(tokens, heads)
    tall = lambda member: member.reshape(tokens, groups, per_group).transpose(1, 0, 2)
    flat = lambda member: member.reshape(tokens, groups, per_group).transpose(1, 2, 0)
    state = final_state(inner, write, tall(step_size * jnp.exp(total_log - from_start)))
    before = incoming_state(state, jnp.repeat(total_log, HDIM), shards)
    left = step_size * jnp.exp(ends[:, None, :] - cumul).reshape(tokens, heads)
    local = local_outputs(
        inner,
        write,
        read,
        tall(cumul),
        flat(cumul),
        flat(step_size),
        tall(left),
        jnp.repeat(d_skip, HDIM).reshape(1, -1),
    )
    return stream_rows, finish(local, read, before, tall(jnp.exp(from_start)), out_gain)


def solution(mesh):
    in_specs = (
        P("tm", None, "head"),
        P("tm"),
        P("tm"),
        P(),
        P(None, None, "head"),
        P("head", None),
        P(None, "head"),
        P(),
        P(None, "head"),
        P(None, "head"),
        P(None, "head"),
        P(None, "head"),
        P("head"),
        P("head"),
        P("head"),
        P("head"),
    )
    out_specs = (P("tm", "head"), P("tm", "head"))
    return jax.shard_map(
        on_device, mesh=mesh, in_specs=in_specs, out_specs=out_specs, check_vma=False
    )
```

```python
import functools
import math

import jax
import jax.numpy as jnp
from jax import lax
from jax.experimental import pallas as pl
from jax.experimental.pallas import tpu as pltpu
from jax.sharding import PartitionSpec as P

GRID = 16
POOL = 4
VHD = 72
HDIM = 64
STATE = 128
CHUNK = 128
LANES = 128

f32 = jnp.float32
bf16 = jnp.bfloat16
VMEM = pltpu.VMEM
CONTRACT_LAST = (((1,), (1,)), ((), ()))
CONTRACT_FIRST = (((0,), (0,)), ((), ()))


def attend_kernel(
    valid_ref, my_ref, full_ref, gain_ref, wqkv_ref, wout_ref, out_ref, normed, context
):
    parts, _, part_width, patch_count = full_ref.shape
    full_width = parts * part_width
    local_width = wqkv_ref.shape[1]
    tokens = patch_count // POOL
    frame = pl.program_id(0)
    pieces = [full_ref[part, 0].astype(f32) for part in range(parts)]
    centre = sum(jnp.sum(piece, axis=0, keepdims=True) for piece in pieces) / full_width
    pieces = [piece - centre for piece in pieces]
    spread = sum(jnp.sum(piece * piece, axis=0, keepdims=True) for piece in pieces) / full_width
    scale = lax.rsqrt(spread + 1e-06)
    for part in range(parts):
        normed[part * part_width : (part + 1) * part_width, :] = (
            pieces[part] * scale * gain_ref[part]
        ).astype(bf16)
    rows = normed[...]
    queries, keys, values = [
        jnp.dot(wqkv_ref[member], rows, preferred_element_type=f32) for member in range(3)
    ]
    key_spot = lax.broadcasted_iota(jnp.int32, (patch_count, patch_count), 0)
    bias = jnp.where(key_spot < valid_ref[frame], 0.0, -1e30).astype(f32)
    factor = VHD ** (-0.5) * math.log2(math.e)
    for head in range(local_width // VHD):
        at = slice(head * VHD, (head + 1) * VHD)
        scores = (
            lax.dot_general(
                keys[at].astype(bf16),
                queries[at].astype(bf16),
                CONTRACT_FIRST,
                preferred_element_type=f32,
            )
            + bias
        )
        powered = jnp.exp2((scores - jnp.max(scores, axis=0, keepdims=True)) * factor)
        total = jnp.sum(powered, axis=0, keepdims=True)
        mixed = jnp.dot(
            values[at].astype(bf16), powered.astype(bf16), preferred_element_type=f32
        )
        context[at, :] = mixed / total
    row = lax.broadcasted_iota(jnp.int32, (tokens, patch_count), 0)
    column = lax.broadcasted_iota(jnp.int32, (tokens, patch_count), 1)
    pooling = jnp.where(column // POOL == row, 1.0 / POOL, 0.0).astype(bf16)
    pooled = lax.dot_general(
        pooling, context[...].astype(bf16), CONTRACT_LAST, preferred_element_type=f32
    ).astype(bf16)
    own = lax.dot_general(
        pooling, full_ref[my_ref[0], 0], CONTRACT_LAST, preferred_element_type=f32
    )
    attended = jnp.dot(pooled, wout_ref[...], preferred_element_type=f32)
    for part in range(parts):
        block = attended[:, part * part_width : (part + 1) * part_width]
        out_ref[part, 0] = (block + jnp.where(my_ref[0] == part, own, 0.0)).astype(bf16)


def attend(full, valid_count, my, gain, w_qkv, w_out):
    parts, frames, part_width, patch_count = full.shape
    width = parts * part_width
    local_width = w_qkv.shape[1]
    tokens = patch_count // POOL
    return pl.pallas_call(
        attend_kernel,
        out_shape=jax.ShapeDtypeStruct((parts, frames, tokens, part_width), bf16),
        grid_spec=pltpu.PrefetchScalarGridSpec(
            num_scalar_prefetch=2,
            grid=(frames,),
            in_specs=[
                pl.BlockSpec((parts, 1, part_width, patch_count), lambda f, *_: (0, f, 0, 0)),
                pl.BlockSpec((parts, part_width, 1), lambda f, *_: (0, 0, 0)),
                pl.BlockSpec((3, local_width, width), lambda f, *_: (0, 0, 0)),
                pl.BlockSpec((local_width, width), lambda f, *_: (0, 0)),
            ],
            out_specs=pl.BlockSpec((parts, 1, tokens, part_width), lambda f, *_: (0, f, 0, 0)),
            scratch_shapes=[
                VMEM((width, patch_count), bf16),
                VMEM((local_width, patch_count), f32),
            ],
        ),
        cost_estimate=pl.CostEstimate(
            flops=frames * patch_count * width * local_width * 10,
            bytes_accessed=12_000_000,
            transcendentals=4_000_000,
        ),
        name="attend",
    )(valid_count, my, full, gain, w_qkv, w_out)


def bucket_kernel(slot_ref, label_ref, count_ref, *refs):
    pieces, out_ref = refs[:-1], refs[-1]
    parts, size, tokens, part_width = pieces[0].shape
    padded = out_ref.shape[2]
    spot = lax.broadcasted_iota(jnp.int32, (tokens, part_width), 0) * POOL

    def step(target, carry):
        slot = slot_ref[target]
        total = jnp.zeros((tokens, part_width), f32)
        for piece, ref in enumerate(pieces):
            inside = jnp.clip(slot - piece * size, 0, size - 1)
            here = sum(ref[part, inside].astype(f32) for part in range(parts))
            total = jnp.where(slot // size == piece, here, total)
        kept = jnp.where(spot < count_ref[target], total, 0.0)
        out_ref[target, :, :part_width] = kept.astype(bf16)
        out_ref[target, :, part_width:] = jnp.full(
            (tokens, padded - part_width), label_ref[target].astype(f32)
        ).astype(bf16)
        return carry

    lax.fori_loop(0, out_ref.shape[0], step, 0)


def bucket(parts, frame_ids, valid_count, shards):
    tokens, part_width = parts[0].shape[2:]
    frames = frame_ids.shape[0]
    padded = (part_width // LANES + 1) * LANES
    onehot = (frame_ids // frames)[None, :] == jnp.arange(shards)[:, None]
    pick = lambda row: jnp.sum(jnp.where(onehot, row[None, :], 0), axis=1).astype(jnp.int32)
    return pl.pallas_call(
        bucket_kernel,
        out_shape=jax.ShapeDtypeStruct((shards, tokens, padded), bf16),
        in_specs=[pl.BlockSpec(memory_space=pltpu.SMEM)] * 3
        + [pl.BlockSpec(memory_space=VMEM)] * len(parts),
        out_specs=pl.BlockSpec(memory_space=VMEM),
        name="bucket",
    )(
        pick(jnp.arange(frames, dtype=jnp.int32)),
        pick(frame_ids % frames + 1),
        pick(valid_count),
        *parts,
    )


def connect_kernel(
    sender_ref, my_ref, arrived_ref, weight_ref, gain_ref, stream_ref, normed_ref, rows, wide
):
    parts, _, tokens, _ = arrived_ref.shape
    width, columns = weight_ref.shape[1:]
    part_width = width // parts
    block_frames = rows.shape[0] // tokens
    for spot in range(block_frames):
        sender = sender_ref[pl.program_id(0) * block_frames + spot]
        for part in range(parts):
            rows[
                spot * tokens : (spot + 1) * tokens, part * part_width : (part + 1) * part_width
            ] = arrived_ref[part, sender, :, :part_width]
    squares = 0.0
    for part in range(parts):
        piece = jnp.dot(rows[...], weight_ref[part], preferred_element_type=f32).astype(bf16)

        @pl.when(my_ref[0] == part)
        def _():
            stream_ref[...] = piece

        piece = piece.astype(f32)
        wide[:, part * columns : (part + 1) * columns] = piece
        squares = squares + jnp.sum(piece * piece, axis=-1, keepdims=True)
    scale = lax.rsqrt(squares / (parts * columns) + 1e-05)
    normed_ref[...] = (wide[...] * scale * gain_ref[...]).astype(bf16)


def connect(arrived, senders, my, weights, norm_gain):
    parts, shards, tokens, padded = arrived.shape
    width, columns = weights.shape[1:]
    frames = senders.shape[0]
    block = math.gcd(frames, 4)
    return pl.pallas_call(
        connect_kernel,
        out_shape=(
            jax.ShapeDtypeStruct((frames * tokens, columns), bf16),
            jax.ShapeDtypeStruct((frames * tokens, parts * columns), bf16),
        ),
        grid_spec=pltpu.PrefetchScalarGridSpec(
            num_scalar_prefetch=2,
            grid=(frames // block,),
            in_specs=[
                pl.BlockSpec((parts, shards, tokens, padded), lambda i, *_: (0, 0, 0, 0)),
                pl.BlockSpec((parts, width, columns), lambda i, *_: (0, 0, 0)),
                pl.BlockSpec((1, parts * columns), lambda i, *_: (0, 0)),
            ],
            out_specs=(
                pl.BlockSpec((block * tokens, columns), lambda i, *_: (i, 0)),
                pl.BlockSpec((block * tokens, parts * columns), lambda i, *_: (i, 0)),
            ),
            scratch_shapes=[
                VMEM((block * tokens, width), bf16),
                VMEM((block * tokens, parts * columns), f32),
            ],
        ),
        name="connect",
    )(senders, my, arrived, weights, norm_gain.reshape(1, -1))


def paired(columns, pair, rows):
    lane = lax.broadcasted_iota(jnp.int32, (rows, LANES), 1)
    return jnp.where(
        lane < HDIM, columns[:, 2 * pair : 2 * pair + 1], columns[:, 2 * pair + 1 : 2 * pair + 2]
    )


def final_state_kernel(inner_ref, write_ref, weight_ref, out_ref):
    length, features = inner_ref.shape
    weights = weight_ref[0]
    for pair in range(features // LANES):
        at = slice(pair * LANES, (pair + 1) * LANES)
        scaled = (inner_ref[:, at].astype(f32) * paired(weights, pair, length)).astype(bf16)
        out_ref[at, :] = lax.dot_general(
            scaled, write_ref[...], CONTRACT_FIRST, preferred_element_type=f32
        ).astype(bf16)


def final_state(inner, write, weights):
    length = inner.shape[0]
    groups = weights.shape[0]
    features = inner.shape[1] // groups
    return pl.pallas_call(
        final_state_kernel,
        out_shape=jax.ShapeDtypeStruct((groups * features, STATE), bf16),
        grid=(groups,),
        in_specs=[
            pl.BlockSpec((length, features), lambda g: (0, g)),
            pl.BlockSpec((length, STATE), lambda g: (0, g)),
            pl.BlockSpec((1, length, weights.shape[2]), lambda g: (g, 0, 0)),
        ],
        out_specs=pl.BlockSpec((features, STATE), lambda g: (g, 0)),
        name="final_state",
    )(inner, write, weights)


def local_kernel(
    inner_ref, write_ref, read_ref, down_ref, across_ref, step_ref, skip_ref, out_ref, state
):
    length, features = inner_ref.shape

    @pl.when(pl.program_id(1) == 0)
    def _():
        state[...] = jnp.zeros_like(state)

    readers, writers = read_ref[...], write_ref[...]
    crossing = lax.dot_general(readers, writers, CONTRACT_LAST, preferred_element_type=f32)
    causal = lax.broadcasted_iota(jnp.int32, (length, length), 0) >= lax.broadcasted_iota(
        jnp.int32, (length, length), 1
    )
    crossing = jnp.where(causal, crossing, 0.0)
    down, across, steps = down_ref[0], across_ref[0], step_ref[0]
    grown = jnp.exp2(down)
    left = jnp.exp2(down[length - 1 :, :] - down)
    lane = lax.broadcasted_iota(jnp.int32, (length, LANES), 1)
    row = lax.broadcasted_iota(jnp.int32, (LANES, STATE), 0)
    for pair in range(features // LANES):
        at = slice(pair * LANES, (pair + 1) * LANES)
        inner = inner_ref[:, at].astype(f32)
        weighted = inner * paired(steps, pair, length)
        stepped = weighted.astype(bf16)
        halves = []
        for head in (2 * pair, 2 * pair + 1):
            spans = jnp.minimum(down[:, head : head + 1] - across[head : head + 1, :], 0.0)
            mixing = crossing * jnp.exp2(spans)
            halves.append(jnp.dot(mixing.astype(bf16), stepped, preferred_element_type=f32))
        held = state[at, :]
        carried = lax.dot_general(
            readers, held.astype(bf16), CONTRACT_LAST, preferred_element_type=f32
        )
        out_ref[:, at] = (
            jnp.where(lane < HDIM, halves[0], halves[1])
            + carried * paired(grown, pair, length)
            + skip_ref[:, at] * inner
        )
        scaled = (weighted * paired(left, pair, length)).astype(bf16)
        last = grown[length - 1 :, :]
        faded = held * jnp.where(
            row < HDIM, last[:, 2 * pair : 2 * pair + 1], last[:, 2 * pair + 1 : 2 * pair + 2]
        )
        state[at, :] = faded + lax.dot_general(
            scaled, writers, CONTRACT_FIRST, preferred_element_type=f32
        )


def local_outputs(inner, write, read, down, across, steps, skip):
    length = inner.shape[0]
    groups, _, per_group = down.shape
    features = inner.shape[1] // groups
    tall = pl.BlockSpec((1, CHUNK, per_group), lambda g, c: (g, c, 0))
    flat = pl.BlockSpec((1, per_group, CHUNK), lambda g, c: (g, 0, c))
    return pl.pallas_call(
        local_kernel,
        out_shape=jax.ShapeDtypeStruct(inner.shape, f32),
        grid=(groups, length // CHUNK),
        in_specs=[
            pl.BlockSpec((CHUNK, features), lambda g, c: (c, g)),
            pl.BlockSpec((CHUNK, STATE), lambda g, c: (c, g)),
            pl.BlockSpec((CHUNK, STATE), lambda g, c: (c, g)),
            tall,
            flat,
            tall,
            pl.BlockSpec((1, features), lambda g, c: (0, g)),
        ],
        out_specs=pl.BlockSpec((CHUNK, features), lambda g, c: (c, g)),
        scratch_shapes=[VMEM((features, STATE), f32)],
        cost_estimate=pl.CostEstimate(
            flops=20_000_000_000, bytes_accessed=20_000_000, transcendentals=4_000_000
        ),
        name="local_outputs",
    )(inner, write, read, down, across, steps, skip)


def prefix_kernel(arrived_ref, decay_ref, out_ref):
    shards, rows, _ = out_ref.shape
    current = jnp.zeros(out_ref.shape[1:], f32)
    for shard in range(shards):
        out_ref[shard] = current.astype(bf16)
        current = decay_ref[shard] * current + arrived_ref[shard, :rows].astype(f32)


def incoming_state(state, row_log, shards):
    rows = state.shape[0] // shards
    room = 8 * LANES
    logs = row_log.reshape(shards, rows)
    high = logs.astype(bf16)
    low = (logs - high.astype(f32)).astype(bf16)
    widen = lambda part: jnp.pad(part, ((0, 0), (0, room - rows))).reshape(shards, 8, LANES)
    outgoing = jnp.concatenate(
        [state.reshape(shards, rows, STATE), widen(high), widen(low)], axis=1
    )
    arrived = lax.all_to_all(outgoing, "tm", split_axis=0, concat_axis=0, tiled=True)
    tail = arrived[:, rows:].astype(f32).reshape(shards, 2, room)[:, :, :rows]
    decay = jnp.exp(tail[:, 0] + tail[:, 1])[:, :, None]
    before = pl.pallas_call(
        prefix_kernel,
        out_shape=jax.ShapeDtypeStruct((shards, rows, STATE), bf16),
        in_specs=[pl.BlockSpec(memory_space=VMEM)] * 2,
        out_specs=pl.BlockSpec(memory_space=VMEM),
        name="prefix",
    )(arrived, decay)
    return lax.all_to_all(before, "tm", split_axis=0, concat_axis=0, tiled=True).reshape(
        shards * rows, STATE
    )


def finish_kernel(local_ref, read_ref, state_ref, grown_ref, gain_ref, out_ref, total):
    length, features = local_ref.shape
    grown = grown_ref[0]
    squares = 0.0
    for pair in range(features // LANES):
        at = slice(pair * LANES, (pair + 1) * LANES)
        carried = lax.dot_general(
            read_ref[...], state_ref[at, :], CONTRACT_LAST, preferred_element_type=f32
        )
        summed = local_ref[:, at] + carried * paired(grown, pair, length)
        total[:, at] = summed
        squares = squares + jnp.sum(summed * summed, axis=-1, keepdims=True)
    scale = lax.rsqrt(squares / features + 1e-05)
    out_ref[...] = (total[...] * scale * gain_ref[...]).astype(bf16)


def finish(local, read, state, grown, out_gain):
    length = local.shape[0]
    groups, _, per_group = grown.shape
    features = local.shape[1] // groups
    block = 2 * CHUNK
    return pl.pallas_call(
        finish_kernel,
        out_shape=jax.ShapeDtypeStruct(local.shape, bf16),
        grid=(groups, length // block),
        in_specs=[
            pl.BlockSpec((block, features), lambda g, c: (c, g)),
            pl.BlockSpec((block, STATE), lambda g, c: (c, g)),
            pl.BlockSpec((features, STATE), lambda g, c: (g, 0)),
            pl.BlockSpec((1, block, per_group), lambda g, c: (g, c, 0)),
            pl.BlockSpec((1, features), lambda g, c: (0, g)),
        ],
        out_specs=pl.BlockSpec((block, features), lambda g, c: (c, g)),
        scratch_shapes=[VMEM((block, features), f32)],
        name="finish",
    )(local, read, state, grown, out_gain.reshape(1, -1))


def on_device(
    patches,
    grid_rows,
    frame_ids,
    ln_gain,
    w_qkv,
    w_out,
    w_conn,
    norm_gain,
    w_x,
    w_b,
    w_c,
    w_dt,
    dt_bias,
    a_log,
    d_skip,
    out_gain,
):
    frame_count, patch_count, part_width = patches.shape
    shards = lax.axis_size("tm")
    my = lax.axis_index("head").astype(jnp.int32).reshape(1)
    sideways = patches.swapaxes(1, 2)
    pieces = 2 if frame_count % 2 == 0 else 1
    size = frame_count // pieces
    cuts = [slice(piece * size, (piece + 1) * size) for piece in range(pieces)]
    gathered = [lax.all_gather(sideways[cut], "head") for cut in cuts]
    all_conn = lax.all_gather(w_conn, "head")
    valid_count = (grid_rows * GRID).astype(jnp.int32)
    gain = ln_gain.reshape(-1, part_width, 1)
    w_across = w_qkv.swapaxes(1, 2)
    parts = [
        lax.all_to_all(
            attend(full, valid_count[cut], my, gain, w_across, w_out),
            "head",
            split_axis=0,
            concat_axis=0,
            tiled=True,
        )
        for cut, full in zip(cuts, gathered)
    ]
    parts, all_conn = lax.optimization_barrier((parts, all_conn))
    outgoing = bucket(parts, frame_ids, valid_count, shards)
    incoming = lax.all_to_all(outgoing, "tm", split_axis=0, concat_axis=0, tiled=True)
    labels = incoming[:, 0, part_width].astype(jnp.int32)
    senders = jnp.sum(
        jnp.where(
            labels[None, :] == jnp.arange(1, frame_count + 1)[:, None],
            jnp.arange(shards, dtype=jnp.int32)[None, :],
            0,
        ),
        axis=1,
    ).astype(jnp.int32)
    arrived = lax.all_gather(incoming, "head")
    stream_rows, normed = connect(arrived, senders, my, all_conn, norm_gain)

    tokens = stream_rows.shape[0]
    heads = w_dt.shape[1]
    groups = w_b.shape[1] // STATE
    per_group = heads // groups
    chunks = tokens // CHUNK
    step_size = jax.nn.softplus(jnp.dot(normed, w_dt, preferred_element_type=f32) + dt_bias)
    log_decay = -jnp.exp(a_log) * step_size
    inner = jnp.dot(normed, w_x, preferred_element_type=f32).astype(bf16)
    write = jnp.dot(normed, w_b, preferred_element_type=f32).astype(bf16)
    read = jnp.dot(normed, w_c, preferred_element_type=f32).astype(bf16)

    cumul = jnp.cumsum(log_decay.reshape(chunks, CHUNK, heads), axis=1)
    ends = cumul[:, -1, :]
    offsets = jnp.cumsum(ends, axis=0) - ends
    total_log = jnp.sum(ends, axis=0)
    from_start = (cumul + offsets[:, None, :]).reshape(tokens, heads)
    tall = lambda member: member.reshape(tokens, groups, per_group).transpose(1, 0, 2)
    flat = lambda member: member.reshape(tokens, groups, per_group).transpose(1, 2, 0)
    state = final_state(inner, write, tall(step_size * jnp.exp(total_log - from_start)))
    before = incoming_state(state, jnp.repeat(total_log, HDIM), shards)
    doubling = cumul * math.log2(math.e)
    local = local_outputs(
        inner,
        write,
        read,
        tall(doubling),
        flat(doubling),
        tall(step_size),
        jnp.repeat(d_skip, HDIM).reshape(1, -1),
    )
    return stream_rows, finish(local, read, before, tall(jnp.exp(from_start)), out_gain)


def solution(mesh):
    in_specs = (
        P("tm", None, "head"),
        P("tm"),
        P("tm"),
        P(),
        P(None, None, "head"),
        P("head", None),
        P(None, "head"),
        P(),
        P(None, "head"),
        P(None, "head"),
        P(None, "head"),
        P(None, "head"),
        P("head"),
        P("head"),
        P("head"),
        P("head"),
    )
    out_specs = (P("tm", "head"), P("tm", "head"))
    return jax.shard_map(
        on_device, mesh=mesh, in_specs=in_specs, out_specs=out_specs, check_vma=False
    )
```

```python
import functools
import math

import jax
import jax.numpy as jnp
from jax import lax
from jax.experimental import pallas as pl
from jax.experimental.pallas import tpu as pltpu
from jax.sharding import PartitionSpec as P

GRID = 16
POOL = 4
VHD = 72
HDIM = 64
STATE = 128
CHUNK = 128
LANES = 128

f32 = jnp.float32
bf16 = jnp.bfloat16
VMEM = pltpu.VMEM
CONTRACT_LAST = (((1,), (1,)), ((), ()))
CONTRACT_FIRST = (((0,), (0,)), ((), ()))


def attend_kernel(
    valid_ref, my_ref, full_ref, gain_ref, wqkv_ref, wout_ref, out_ref, normed, context
):
    parts, _, part_width, patch_count = full_ref.shape
    full_width = parts * part_width
    local_width = wqkv_ref.shape[1]
    tokens = patch_count // POOL
    frame = pl.program_id(0)
    pieces = [full_ref[part, 0].astype(f32) for part in range(parts)]
    centre = sum(jnp.sum(piece, axis=0, keepdims=True) for piece in pieces) / full_width
    pieces = [piece - centre for piece in pieces]
    spread = sum(jnp.sum(piece * piece, axis=0, keepdims=True) for piece in pieces) / full_width
    scale = lax.rsqrt(spread + 1e-06)
    for part in range(parts):
        normed[part * part_width : (part + 1) * part_width, :] = (
            pieces[part] * scale * gain_ref[part]
        ).astype(bf16)
    rows = normed[...]
    queries, keys, values = [
        jnp.dot(wqkv_ref[member], rows, preferred_element_type=f32) for member in range(3)
    ]
    key_spot = lax.broadcasted_iota(jnp.int32, (patch_count, patch_count), 0)
    bias = jnp.where(key_spot < valid_ref[frame], 0.0, -1e30).astype(f32)
    factor = VHD ** (-0.5) * math.log2(math.e)
    for head in range(local_width // VHD):
        at = slice(head * VHD, (head + 1) * VHD)
        scores = (
            lax.dot_general(
                keys[at].astype(bf16),
                queries[at].astype(bf16),
                CONTRACT_FIRST,
                preferred_element_type=f32,
            )
            + bias
        )
        powered = jnp.exp2((scores - jnp.max(scores, axis=0, keepdims=True)) * factor)
        total = jnp.sum(powered, axis=0, keepdims=True)
        mixed = jnp.dot(
            values[at].astype(bf16), powered.astype(bf16), preferred_element_type=f32
        )
        context[at, :] = mixed * (1.0 / total)
    row = lax.broadcasted_iota(jnp.int32, (tokens, patch_count), 0)
    column = lax.broadcasted_iota(jnp.int32, (tokens, patch_count), 1)
    pooling = jnp.where(column // POOL == row, 1.0 / POOL, 0.0).astype(bf16)
    pooled = lax.dot_general(
        pooling, context[...].astype(bf16), CONTRACT_LAST, preferred_element_type=f32
    ).astype(bf16)
    own = lax.dot_general(
        pooling, full_ref[my_ref[0], 0], CONTRACT_LAST, preferred_element_type=f32
    )
    attended = jnp.dot(pooled, wout_ref[...], preferred_element_type=f32)
    for part in range(parts):
        block = attended[:, part * part_width : (part + 1) * part_width]
        out_ref[part, 0] = (block + jnp.where(my_ref[0] == part, own, 0.0)).astype(bf16)


def attend(full, valid_count, my, gain, w_qkv, w_out):
    parts, frames, part_width, patch_count = full.shape
    width = parts * part_width
    local_width = w_qkv.shape[1]
    tokens = patch_count // POOL
    return pl.pallas_call(
        attend_kernel,
        out_shape=jax.ShapeDtypeStruct((parts, frames, tokens, part_width), bf16),
        grid_spec=pltpu.PrefetchScalarGridSpec(
            num_scalar_prefetch=2,
            grid=(frames,),
            in_specs=[
                pl.BlockSpec((parts, 1, part_width, patch_count), lambda f, *_: (0, f, 0, 0)),
                pl.BlockSpec((parts, part_width, 1), lambda f, *_: (0, 0, 0)),
                pl.BlockSpec((3, local_width, width), lambda f, *_: (0, 0, 0)),
                pl.BlockSpec((local_width, width), lambda f, *_: (0, 0)),
            ],
            out_specs=pl.BlockSpec((parts, 1, tokens, part_width), lambda f, *_: (0, f, 0, 0)),
            scratch_shapes=[
                VMEM((width, patch_count), bf16),
                VMEM((local_width, patch_count), f32),
            ],
        ),
        cost_estimate=pl.CostEstimate(
            flops=frames * patch_count * width * local_width * 10,
            bytes_accessed=12_000_000,
            transcendentals=4_000_000,
        ),
        name="attend",
    )(valid_count, my, full, gain, w_qkv, w_out)


def bucket_kernel(slot_ref, label_ref, count_ref, *refs):
    pieces, out_ref = refs[:-1], refs[-1]
    parts, _, tokens, part_width = pieces[0].shape
    padded = out_ref.shape[2]
    spot = lax.broadcasted_iota(jnp.int32, (tokens, part_width), 0) * POOL

    def step(target, carry):
        slot = slot_ref[target]
        total = jnp.zeros((tokens, part_width), f32)
        start = 0
        for ref in pieces:
            inside = jnp.clip(slot - start, 0, ref.shape[1] - 1)
            here = sum(ref[part, inside].astype(f32) for part in range(parts))
            total = jnp.where(slot >= start, here, total)
            start += ref.shape[1]
        kept = jnp.where(spot < count_ref[target], total, 0.0)
        out_ref[target, :, :part_width] = kept.astype(bf16)
        out_ref[target, :, part_width:] = jnp.full(
            (tokens, padded - part_width), label_ref[target].astype(f32)
        ).astype(bf16)
        return carry

    lax.fori_loop(0, out_ref.shape[0], step, 0)


def bucket(parts, frame_ids, valid_count, shards):
    tokens, part_width = parts[0].shape[2:]
    frames = frame_ids.shape[0]
    padded = (part_width // LANES + 1) * LANES
    onehot = (frame_ids // frames)[None, :] == jnp.arange(shards)[:, None]
    pick = lambda row: jnp.sum(jnp.where(onehot, row[None, :], 0), axis=1).astype(jnp.int32)
    return pl.pallas_call(
        bucket_kernel,
        out_shape=jax.ShapeDtypeStruct((shards, tokens, padded), bf16),
        in_specs=[pl.BlockSpec(memory_space=pltpu.SMEM)] * 3
        + [pl.BlockSpec(memory_space=VMEM)] * len(parts),
        out_specs=pl.BlockSpec(memory_space=VMEM),
        name="bucket",
    )(
        pick(jnp.arange(frames, dtype=jnp.int32)),
        pick(frame_ids % frames + 1),
        pick(valid_count),
        *parts,
    )


def connect_kernel(
    sender_ref, my_ref, arrived_ref, weight_ref, gain_ref, stream_ref, normed_ref, rows, wide
):
    parts, _, tokens, _ = arrived_ref.shape
    width, columns = weight_ref.shape[1:]
    part_width = width // parts
    block_frames = rows.shape[0] // tokens
    for spot in range(block_frames):
        sender = sender_ref[pl.program_id(0) * block_frames + spot]
        for part in range(parts):
            rows[
                spot * tokens : (spot + 1) * tokens, part * part_width : (part + 1) * part_width
            ] = arrived_ref[part, sender, :, :part_width]
    squares = 0.0
    for part in range(parts):
        piece = jnp.dot(rows[...], weight_ref[part], preferred_element_type=f32).astype(bf16)

        @pl.when(my_ref[0] == part)
        def _():
            stream_ref[...] = piece

        piece = piece.astype(f32)
        wide[:, part * columns : (part + 1) * columns] = piece
        squares = squares + jnp.sum(piece * piece, axis=-1, keepdims=True)
    scale = lax.rsqrt(squares / (parts * columns) + 1e-05)
    normed_ref[...] = (wide[...] * scale * gain_ref[...]).astype(bf16)


def connect(arrived, senders, my, weights, norm_gain):
    parts, shards, tokens, padded = arrived.shape
    width, columns = weights.shape[1:]
    frames = senders.shape[0]
    block = math.gcd(frames, 4)
    return pl.pallas_call(
        connect_kernel,
        out_shape=(
            jax.ShapeDtypeStruct((frames * tokens, columns), bf16),
            jax.ShapeDtypeStruct((frames * tokens, parts * columns), bf16),
        ),
        grid_spec=pltpu.PrefetchScalarGridSpec(
            num_scalar_prefetch=2,
            grid=(frames // block,),
            in_specs=[
                pl.BlockSpec((parts, shards, tokens, padded), lambda i, *_: (0, 0, 0, 0)),
                pl.BlockSpec((parts, width, columns), lambda i, *_: (0, 0, 0)),
                pl.BlockSpec((1, parts * columns), lambda i, *_: (0, 0)),
            ],
            out_specs=(
                pl.BlockSpec((block * tokens, columns), lambda i, *_: (i, 0)),
                pl.BlockSpec((block * tokens, parts * columns), lambda i, *_: (i, 0)),
            ),
            scratch_shapes=[
                VMEM((block * tokens, width), bf16),
                VMEM((block * tokens, parts * columns), f32),
            ],
        ),
        name="connect",
    )(senders, my, arrived, weights, norm_gain.reshape(1, -1))


def paired(columns, pair, rows):
    lane = lax.broadcasted_iota(jnp.int32, (rows, LANES), 1)
    return jnp.where(
        lane < HDIM, columns[:, 2 * pair : 2 * pair + 1], columns[:, 2 * pair + 1 : 2 * pair + 2]
    )


def final_state_kernel(inner_ref, write_ref, weight_ref, out_ref, scaled):
    length, features = inner_ref.shape
    weights = weight_ref[0]
    for pair in range(features // LANES):
        at = slice(pair * LANES, (pair + 1) * LANES)
        scaled[:, at] = (inner_ref[:, at].astype(f32) * paired(weights, pair, length)).astype(bf16)
    sideways = lax.dot_general(
        write_ref[...], scaled[...], CONTRACT_FIRST, preferred_element_type=f32
    )
    out_ref[...] = sideways.T.astype(bf16)


def final_state(inner, write, weights):
    length = inner.shape[0]
    groups = weights.shape[0]
    features = inner.shape[1] // groups
    return pl.pallas_call(
        final_state_kernel,
        out_shape=jax.ShapeDtypeStruct((groups * features, STATE), bf16),
        grid=(groups,),
        in_specs=[
            pl.BlockSpec((length, features), lambda g: (0, g)),
            pl.BlockSpec((length, STATE), lambda g: (0, g)),
            pl.BlockSpec((1, length, weights.shape[2]), lambda g: (g, 0, 0)),
        ],
        out_specs=pl.BlockSpec((features, STATE), lambda g: (g, 0)),
        scratch_shapes=[VMEM((length, features), bf16)],
        name="final_state",
    )(inner, write, weights)


def local_kernel(
    inner_ref, write_ref, read_ref, down_ref, across_ref, step_ref, skip_ref, out_ref, state, scaled
):
    length, features = inner_ref.shape

    @pl.when(pl.program_id(1) == 0)
    def _():
        state[...] = jnp.zeros_like(state)

    readers, writers = read_ref[...], write_ref[...]
    crossing = lax.dot_general(readers, writers, CONTRACT_LAST, preferred_element_type=f32)
    causal = lax.broadcasted_iota(jnp.int32, (length, length), 0) >= lax.broadcasted_iota(
        jnp.int32, (length, length), 1
    )
    crossing = jnp.where(causal, crossing, 0.0)
    down, across, steps = down_ref[0], across_ref[0], step_ref[0]
    grown = jnp.exp2(down)
    left = jnp.exp2(down[length - 1 :, :] - down)
    lane = lax.broadcasted_iota(jnp.int32, (length, LANES), 1)
    held = state[...]
    carried = jnp.dot(readers, held.astype(bf16), preferred_element_type=f32)
    for pair in range(features // LANES):
        at = slice(pair * LANES, (pair + 1) * LANES)
        inner = inner_ref[:, at].astype(f32)
        weighted = inner * paired(steps, pair, length)
        halves = []
        for head in (2 * pair, 2 * pair + 1):
            spans = jnp.minimum(down[:, head : head + 1] - across[head : head + 1, :], 0.0)
            halves.append((crossing * jnp.exp2(spans)).astype(bf16))
        stacked = jnp.concatenate(
            [jnp.where(lane < HDIM, weighted, 0.0), jnp.where(lane < HDIM, 0.0, weighted)], axis=0
        ).astype(bf16)
        within = jnp.dot(
            jnp.concatenate(halves, axis=1), stacked, preferred_element_type=f32
        )
        faded = paired(grown, pair, length)
        out_ref[:, at] = within + carried[:, at] * faded + skip_ref[:, at] * inner
        scaled[:, at] = (weighted * paired(left, pair, length)).astype(bf16)
        state[:, at] = held[:, at] * faded[length - 1 :, :]
    state[...] += lax.dot_general(
        writers, scaled[...], CONTRACT_FIRST, preferred_element_type=f32
    )


def local_outputs(inner, write, read, down, across, steps, skip):
    length = inner.shape[0]
    groups, _, per_group = down.shape
    features = inner.shape[1] // groups
    tall = pl.BlockSpec((1, CHUNK, per_group), lambda g, c: (g, c, 0))
    flat = pl.BlockSpec((1, per_group, CHUNK), lambda g, c: (g, 0, c))
    return pl.pallas_call(
        local_kernel,
        out_shape=jax.ShapeDtypeStruct(inner.shape, f32),
        grid=(groups, length // CHUNK),
        in_specs=[
            pl.BlockSpec((CHUNK, features), lambda g, c: (c, g)),
            pl.BlockSpec((CHUNK, STATE), lambda g, c: (c, g)),
            pl.BlockSpec((CHUNK, STATE), lambda g, c: (c, g)),
            tall,
            flat,
            tall,
            pl.BlockSpec((1, features), lambda g, c: (0, g)),
        ],
        out_specs=pl.BlockSpec((CHUNK, features), lambda g, c: (c, g)),
        scratch_shapes=[VMEM((STATE, features), f32), VMEM((CHUNK, features), bf16)],
        cost_estimate=pl.CostEstimate(
            flops=20_000_000_000, bytes_accessed=20_000_000, transcendentals=4_000_000
        ),
        name="local_outputs",
    )(inner, write, read, down, across, steps, skip)


def prefix_kernel(arrived_ref, decay_ref, out_ref):
    shards, rows, _ = out_ref.shape
    current = jnp.zeros(out_ref.shape[1:], f32)
    for shard in range(shards):
        out_ref[shard] = current.astype(bf16)
        current = decay_ref[shard] * current + arrived_ref[shard, :rows].astype(f32)


def incoming_state(state, row_log, shards):
    rows = state.shape[0] // shards
    room = 8 * LANES
    logs = row_log.reshape(shards, rows)
    high = logs.astype(bf16)
    low = (logs - high.astype(f32)).astype(bf16)
    widen = lambda part: jnp.pad(part, ((0, 0), (0, room - rows))).reshape(shards, 8, LANES)
    outgoing = jnp.concatenate(
        [state.reshape(shards, rows, STATE), widen(high), widen(low)], axis=1
    )
    arrived = lax.all_to_all(outgoing, "tm", split_axis=0, concat_axis=0, tiled=True)
    tail = arrived[:, rows:].astype(f32).reshape(shards, 2, room)[:, :, :rows]
    decay = jnp.exp(tail[:, 0] + tail[:, 1])[:, :, None]
    before = pl.pallas_call(
        prefix_kernel,
        out_shape=jax.ShapeDtypeStruct((shards, rows, STATE), bf16),
        in_specs=[pl.BlockSpec(memory_space=VMEM)] * 2,
        out_specs=pl.BlockSpec(memory_space=VMEM),
        name="prefix",
    )(arrived, decay)
    return lax.all_to_all(before, "tm", split_axis=0, concat_axis=0, tiled=True).reshape(
        shards * rows, STATE
    )


def finish_kernel(local_ref, read_ref, state_ref, grown_ref, gain_ref, out_ref, total):
    length, features = local_ref.shape
    grown = grown_ref[0]
    squares = 0.0
    carried = lax.dot_general(
        read_ref[...], state_ref[...], CONTRACT_LAST, preferred_element_type=f32
    )
    for pair in range(features // LANES):
        at = slice(pair * LANES, (pair + 1) * LANES)
        summed = local_ref[:, at] + carried[:, at] * paired(grown, pair, length)
        total[:, at] = summed
        squares = squares + jnp.sum(summed * summed, axis=-1, keepdims=True)
    scale = lax.rsqrt(squares / features + 1e-05)
    out_ref[...] = (total[...] * scale * gain_ref[...]).astype(bf16)


def finish(local, read, state, grown, out_gain):
    length = local.shape[0]
    groups, _, per_group = grown.shape
    features = local.shape[1] // groups
    block = 2 * CHUNK
    return pl.pallas_call(
        finish_kernel,
        out_shape=jax.ShapeDtypeStruct(local.shape, bf16),
        grid=(groups, length // block),
        in_specs=[
            pl.BlockSpec((block, features), lambda g, c: (c, g)),
            pl.BlockSpec((block, STATE), lambda g, c: (c, g)),
            pl.BlockSpec((features, STATE), lambda g, c: (g, 0)),
            pl.BlockSpec((1, block, per_group), lambda g, c: (g, c, 0)),
            pl.BlockSpec((1, features), lambda g, c: (0, g)),
        ],
        out_specs=pl.BlockSpec((block, features), lambda g, c: (c, g)),
        scratch_shapes=[VMEM((block, features), f32)],
        name="finish",
    )(local, read, state, grown, out_gain.reshape(1, -1))


def on_device(
    patches,
    grid_rows,
    frame_ids,
    ln_gain,
    w_qkv,
    w_out,
    w_conn,
    norm_gain,
    w_x,
    w_b,
    w_c,
    w_dt,
    dt_bias,
    a_log,
    d_skip,
    out_gain,
):
    frame_count, patch_count, part_width = patches.shape
    shards = lax.axis_size("tm")
    my = lax.axis_index("head").astype(jnp.int32).reshape(1)
    sideways = patches.swapaxes(1, 2)
    first = max(frame_count // 4, 1)
    cuts = [cut for cut in (slice(0, first), slice(first, frame_count)) if cut.start < cut.stop]
    gathered = [lax.all_gather(sideways[cut], "head") for cut in cuts]
    all_conn = lax.all_gather(w_conn, "head")
    valid_count = (grid_rows * GRID).astype(jnp.int32)
    gain = ln_gain.reshape(-1, part_width, 1)
    w_across = w_qkv.swapaxes(1, 2)
    parts = [
        lax.all_to_all(
            attend(full, valid_count[cut], my, gain, w_across, w_out),
            "head",
            split_axis=0,
            concat_axis=0,
            tiled=True,
        )
        for cut, full in zip(cuts, gathered)
    ]
    parts, all_conn = lax.optimization_barrier((parts, all_conn))
    outgoing = bucket(parts, frame_ids, valid_count, shards)
    incoming = lax.all_to_all(outgoing, "tm", split_axis=0, concat_axis=0, tiled=True)
    labels = incoming[:, 0, part_width].astype(jnp.int32)
    senders = jnp.sum(
        jnp.where(
            labels[None, :] == jnp.arange(1, frame_count + 1)[:, None],
            jnp.arange(shards, dtype=jnp.int32)[None, :],
            0,
        ),
        axis=1,
    ).astype(jnp.int32)
    arrived = lax.all_gather(incoming, "head")
    stream_rows, normed = connect(arrived, senders, my, all_conn, norm_gain)

    tokens = stream_rows.shape[0]
    heads = w_dt.shape[1]
    groups = w_b.shape[1] // STATE
    per_group = heads // groups
    chunks = tokens // CHUNK
    step_size = jax.nn.softplus(jnp.dot(normed, w_dt, preferred_element_type=f32) + dt_bias)
    log_decay = -jnp.exp(a_log) * step_size
    inner = jnp.dot(normed, w_x, preferred_element_type=f32).astype(bf16)
    write = jnp.dot(normed, w_b, preferred_element_type=f32).astype(bf16)
    read = jnp.dot(normed, w_c, preferred_element_type=f32).astype(bf16)

    cumul = jnp.cumsum(log_decay.reshape(chunks, CHUNK, heads), axis=1)
    ends = cumul[:, -1, :]
    offsets = jnp.cumsum(ends, axis=0) - ends
    total_log = jnp.sum(ends, axis=0)
    from_start = (cumul + offsets[:, None, :]).reshape(tokens, heads)
    tall = lambda member: member.reshape(tokens, groups, per_group).transpose(1, 0, 2)
    flat = lambda member: member.reshape(tokens, groups, per_group).transpose(1, 2, 0)
    state = final_state(inner, write, tall(step_size * jnp.exp(total_log - from_start)))
    before = incoming_state(state, jnp.repeat(total_log, HDIM), shards)
    doubling = cumul * math.log2(math.e)
    local = local_outputs(
        inner,
        write,
        read,
        tall(doubling),
        flat(doubling),
        tall(step_size),
        jnp.repeat(d_skip, HDIM).reshape(1, -1),
    )
    return stream_rows, finish(local, read, before, tall(jnp.exp(from_start)), out_gain)


def solution(mesh):
    in_specs = (
        P("tm", None, "head"),
        P("tm"),
        P("tm"),
        P(),
        P(None, None, "head"),
        P("head", None),
        P(None, "head"),
        P(),
        P(None, "head"),
        P(None, "head"),
        P(None, "head"),
        P(None, "head"),
        P("head"),
        P("head"),
        P("head"),
        P("head"),
    )
    out_specs = (P("tm", "head"), P("tm", "head"))
    return jax.shard_map(
        on_device, mesh=mesh, in_specs=in_specs, out_specs=out_specs, check_vma=False
    )
```
